512 devices in a mesh: grp: 16 (over z, core), sp: 32 (over x, y).
Axes of the slice: x: 4, y: 8, z: 8, core: 2. Of those that a mesh axis runs over, the one named last changes fastest.
Arguments:
- query_input: bfloat16 [65536, 4096], P(('grp', 'sp')), may hold values from -6 to 6
- key_input: bfloat16 [65536, 4096], P(('grp', 'sp')), may hold values from -6 to 6
- value_heads_input: bfloat16 [65536, 4096], P(('grp', 'sp')), may hold values from -6 to 6
- conv_weight: float32 [3, 4, 4096], P(None, None, 'sp'), may hold values from -3 to 3
- feature_map: bfloat16 [128, 1024], replicated, may hold values from -0.5 to 0.5
- out_gain: float32 [4096], P('sp'), may hold values from 0.25 to 1.75
Outputs:
- attended: bfloat16 [65536, 4096], P(('grp', 'sp'))
The draws below stay inside these ranges and needn't reach their ends.
All inputs are finite; a program needn't handle non-finite values.
Results may differ from the reference program's by a relative error of at most 0.0052.
Values may be sent and summed in bfloat16 or wider, within the bound.
A program may use at most 128 MiB of HBM per device.

```python
import jax
import jax.numpy as jnp
from jax import lax

H = 32
DH = 128
M = 1024
CONV = 4
BLOCK = 256
D = 4096
TOKEN_COUNT = 65536


def block_scale(stream_key, extent, shards, smallest, top_value):
    loudness = 1.0
    for position, shards_of in shards:
        steps = jax.random.uniform(jax.random.fold_in(jax.random.fold_in(stream_key, 6), position), (shards_of,), jnp.float32, smallest / len(shards), top_value / len(shards))
        loudness = loudness * jnp.repeat(jnp.exp(steps), extent[position] // shards_of).reshape((-1,) + (1,) * (len(extent) - 1 - position))
    return loudness


def noise(stream_key, extent, width, bound, split=(), held_as=jnp.bfloat16):
    array = width * jax.random.normal(stream_key, extent, jnp.float32)
    if split:
        array = array * block_scale(stream_key, extent, split, -0.22, 0.18)
    return jnp.clip(array, -bound, bound).astype(held_as)


def setup_inputs(seed: int = 0) -> dict:
    key_of = jax.random.split(jax.random.key(seed), 7)
    query_input = noise(key_of[0], (TOKEN_COUNT, D), 1.0, 6.0, ((0, 512),))
    key_input = noise(key_of[1], (TOKEN_COUNT, D), 1.0, 6.0, ((0, 512),))
    value_heads_input = noise(key_of[2], (TOKEN_COUNT, D), 1.0, 6.0, ((0, 512),))
    conv_weight = noise(key_of[3], (3, CONV, D), 0.5, 3.0, ((2, 32),), jnp.float32)
    feature_map = noise(key_of[4], (DH, M), DH ** -0.5, 0.5)
    out_gain = jnp.clip(1.0 + 0.15 * jax.random.normal(key_of[5], (D,), jnp.float32), 0.25, 1.75)
    return {"query_input": query_input, "key_input": key_input, "value_heads_input": value_heads_input, "conv_weight": conv_weight, "feature_map": feature_map, "out_gain": out_gain}


def causal_conv(source, earlier, weights):
    tap_count = weights.shape[0]
    length = source.shape[0]
    padded = jnp.concatenate([earlier.astype(jnp.float32), source.astype(jnp.float32)], 0)
    summed = jnp.zeros(source.shape, jnp.float32)
    for tap_index in range(tap_count):
        row_begin = tap_count - 1 - tap_index
        summed = summed + weights[tap_index] * padded[row_begin:row_begin + length]
    return summed.astype(jnp.bfloat16)

def reference(query_input, key_input, value_heads_input, conv_weight, feature_map, out_gain):

    def by_head(matrix):
        return matrix.reshape(TOKEN_COUNT, H, DH).transpose(1, 0, 2)
    weights_all = conv_weight.reshape(3, CONV, H, DH).transpose(2, 0, 1, 3)
    gain_table = out_gain.reshape(H, DH)
    causal_mask = lax.iota(jnp.int32, BLOCK)[None, :] <= lax.iota(jnp.int32, BLOCK)[:, None]
    block_count = TOKEN_COUNT // BLOCK

    def one_head(inputs):
        query_head, key_head, value_head, weights, gain_head = inputs
        zero_rim = jnp.zeros((CONV - 1, DH), jnp.bfloat16)
        sources = (query_head, key_head, value_head)
        blocked = tuple((causal_conv(sources[member], zero_rim, weights[member]).reshape(block_count, BLOCK, DH) for member in range(3)))

        def block_step(kv_state, block_in):
            query_block, key_block, value_tile_rows = block_in
            query_featurized = jnp.maximum(jnp.dot(query_block, feature_map, preferred_element_type=jnp.float32), 0.0).astype(jnp.bfloat16)
            key_featurized = jnp.maximum(jnp.dot(key_block, feature_map, preferred_element_type=jnp.float32), 0.0).astype(jnp.bfloat16)
            scores = jnp.dot(query_featurized, key_featurized.T, preferred_element_type=jnp.float32)
            scores = jnp.where(causal_mask, scores, 0.0).astype(jnp.bfloat16)
            local_part = jnp.dot(scores, value_tile_rows, preferred_element_type=jnp.float32)
            carried_part = jnp.dot(query_featurized.astype(jnp.float32), kv_state, precision=lax.Precision.HIGHEST)
            numerator = local_part + carried_part
            kv_state = kv_state + jnp.dot(key_featurized.T, value_tile_rows, preferred_element_type=jnp.float32)
            normed = numerator * lax.rsqrt(lax.optimization_barrier(jnp.mean(numerator * numerator, -1, keepdims=True)) + 1e-06) * gain_head
            return (kv_state, normed.astype(jnp.bfloat16))
        _, outputs = lax.scan(block_step, jnp.zeros((M, DH), jnp.float32), blocked)
        return outputs.reshape(TOKEN_COUNT, DH)
    heads_out = lax.map(one_head, (by_head(query_input), by_head(key_input), by_head(value_heads_input), weights_all, gain_table))
    return heads_out.transpose(1, 0, 2).reshape(TOKEN_COUNT, H * DH)
```

```python
import functools

import jax
import jax.numpy as jnp
from jax import lax
from jax.experimental import pallas as pl
from jax.experimental.pallas import tpu as pltpu
from jax.sharding import PartitionSpec as P

DH = 128
CONV = 4
BLOCK = 256
CHUNK = 128
HALO = 16
MESH = pl.DeviceIdType.MESH
F32 = jnp.float32
BF16 = jnp.bfloat16
CONTRACT_LAST = (((1,), (1,)), ((), ()))
CONTRACT_FIRST = (((0,), (0,)), ((), ()))
Q, K, V = 0, 1, 2


def kernel(
    nsp,
    ngrp,
    q_hbm,
    k_hbm,
    v_hbm,
    cw_ref,
    fm_ref,
    gain_ref,
    out_hbm,
    qbuf,
    kbuf,
    vbuf,
    qf,
    kf,
    vc,
    upd,
    loc,
    obuf,
    total,
    tsend,
    tin,
    psend,
    prx,
    esend,
    ein,
    est,
    in_send,
    in_recv,
    halo_send,
    halo_recv,
    core_send,
    core_recv,
    z_send,
    z_recv,
    out_send,
    out_recv,
):
    nb = nsp // 2
    nz = ngrp // 2
    m = fm_ref.shape[1]
    me = lax.axis_index("sp")
    g = lax.axis_index("grp")
    z, core = g // 2, lax.rem(g, 2)
    b0 = me // 2
    partner = g + 1 - 2 * core
    following = lax.rem(g + 1, ngrp)
    hbm = (q_hbm, k_hbm, v_hbm)
    bufs = (qbuf, kbuf, vbuf)

    barrier = pltpu.get_barrier_semaphore()

    @pl.loop(1, nsp)
    def _(i):
        pl.semaphore_signal(
            barrier, inc=1, device_id={"sp": lax.rem(me + i, nsp)}, device_id_type=MESH
        )

    @pl.loop(1, ngrp)
    def _(i):
        pl.semaphore_signal(
            barrier, inc=1, device_id={"grp": lax.rem(g + i, ngrp)}, device_id_type=MESH
        )

    pl.semaphore_wait(barrier, nsp + ngrp - 2)

    def rows_of(chunk):
        return pl.ds(pl.multiple_of(HALO + chunk * CHUNK, 16), CHUNK)

    def columns_of(head):
        return pl.ds(pl.multiple_of(head * DH, DH), DH)

    def input_copy(t, d):
        return pltpu.make_async_remote_copy(
            src_ref=hbm[t].at[:, columns_of(d)],
            dst_ref=bufs[t].at[rows_of(me)],
            send_sem=in_send.at[t, d],
            recv_sem=in_recv.at[t, me],
            device_id={"sp": d},
            device_id_type=MESH,
        )

    def own_copy(t):
        return pltpu.make_async_copy(
            hbm[t].at[:, columns_of(me)], bufs[t].at[rows_of(me)], in_recv.at[t, me]
        )

    def send_inputs(tensors):
        for t in tensors:
            own_copy(t).start()
        for t in tensors:
            input_copy(t, me + 1 - 2 * lax.rem(me, 2)).start()

        @pl.loop(1, nb)
        def _(i):
            pair = lax.rem(b0 + nb - i, nb)
            for e in range(2):
                for t in tensors:
                    input_copy(t, 2 * pair + e).start()

    def halo_copy(t):
        return pltpu.make_async_remote_copy(
            src_ref=bufs[t].at[pl.ds(nsp * CHUNK, HALO)],
            dst_ref=bufs[t].at[pl.ds(0, HALO)],
            send_sem=halo_send.at[t],
            recv_sem=halo_recv.at[t],
            device_id={"grp": following},
            device_id_type=MESH,
        )

    def arrive(b, tensors):
        for t in tensors:
            for e in range(2):
                rows = bufs[t].at[rows_of(2 * b + e)]
                pltpu.make_async_copy(rows, rows, in_recv.at[t, 2 * b + e]).wait()

        @pl.when(b == nb - 1)
        def _():
            for t in tensors:
                halo_copy(t).start()

    def halo_ready(b, tensors):
        @pl.when(b == 0)
        def _():
            for t in tensors:
                halo_copy(t).wait_recv()

            @pl.when(g == 0)
            def _():
                for t in tensors:
                    bufs[t][pl.ds(0, HALO), :] = jnp.zeros((HALO, DH), BF16)

    def conv(t, b):
        rows = bufs[t][pl.ds(pl.multiple_of(b * BLOCK, BLOCK), BLOCK + HALO), :].astype(F32)
        summed = cw_ref[t, 0:1, :] * rows[HALO:]
        for j in range(1, CONV):
            summed = summed + cw_ref[t, j : j + 1, :] * pltpu.roll(rows, j, 0)[HALO:]
        return summed.astype(BF16)

    def featurize(rows, dst, b):
        for j in range(0, m, 256):
            f = jnp.dot(rows, fm_ref[:, j : j + 256], preferred_element_type=F32)
            dst[b, :, j : j + 256] = jnp.maximum(f, 0.0).astype(BF16)

    def block_rows(b):
        return pl.ds(pl.multiple_of(b * BLOCK, BLOCK), BLOCK)

    send_inputs((K, V))
    send_inputs((Q,))

    total[...] = jnp.zeros_like(total)

    def key_block(b):
        halo_ready(b, (K, V))
        value = conv(V, b)
        vc[block_rows(b), :] = value
        featurize(conv(K, b), kf, b)
        increment = lax.dot_general(value, kf[b], CONTRACT_FIRST, preferred_element_type=F32)
        upd[b] = increment
        total[...] += increment

    arrive(b0, (K, V))

    @pl.loop(1, nb)
    def _(i):
        b = lax.rem(b0 + i, nb)
        arrive(b, (K, V))
        key_block(b)

    key_block(b0)

    half = DH // 2
    mine = pl.ds(pl.multiple_of(core * half, half), half)
    theirs = pl.ds(pl.multiple_of((1 - core) * half, half), half)

    def core_copy(k, src, dst):
        return pltpu.make_async_remote_copy(
            src_ref=src,
            dst_ref=dst,
            send_sem=core_send.at[k],
            recv_sem=core_recv.at[k],
            device_id={"grp": partner},
            device_id_type=MESH,
        )

    tsend[...] = total[theirs, :].astype(BF16)
    first = core_copy(0, tsend, tin)
    first.start()

    def exclusive(b, running):
        increment = upd[b]
        upd[b] = est[...]
        est[...] += increment
        return running

    est[...] = jnp.zeros_like(est)
    lax.fori_loop(0, nb, exclusive, 0)

    first.wait_recv()
    psend[...] = (total[mine, :] + tin[...].astype(F32)).astype(BF16)

    def z_copy(to):
        return pltpu.make_async_remote_copy(
            src_ref=psend,
            dst_ref=prx.at[z],
            send_sem=z_send.at[to],
            recv_sem=z_recv.at[z],
            device_id={"grp": 2 * to + core},
            device_id_type=MESH,
        )

    @pl.loop(1, nz)
    def _(i):
        @pl.when(z + i < nz)
        def _():
            z_copy(z + i).start()

    row_at = lax.broadcasted_iota(jnp.int32, (BLOCK, BLOCK), 0)
    column_at = lax.broadcasted_iota(jnp.int32, (BLOCK, BLOCK), 1)

    def query_block(b):
        halo_ready(b, (Q,))
        featurize(conv(Q, b), qf, b)
        scores = lax.dot_general(qf[b], kf[b], CONTRACT_LAST, preferred_element_type=F32)
        scores = jnp.where(column_at <= row_at, scores, 0.0).astype(BF16)
        loc[block_rows(b), :] = jnp.dot(
            scores, vc[block_rows(b), :], preferred_element_type=F32
        )

    arrive(b0, (Q,))

    @pl.loop(1, nb)
    def _(i):
        b = lax.rem(b0 + i, nb)
        arrive(b, (Q,))
        query_block(b)

    query_block(b0)

    est[mine, :] = jnp.zeros((half, m), F32)

    @pl.loop(0, nz)
    def _(i):
        @pl.when(i < z)
        def _():
            slot = prx.at[i]
            pltpu.make_async_copy(slot, slot, z_recv.at[i]).wait()
            est[mine, :] += prx[i].astype(F32)

    @pl.when(core == 0)
    def _():
        esend[...] = (est[mine, :] + total[mine, :]).astype(BF16)

    @pl.when(core == 1)
    def _():
        esend[...] = est[mine, :].astype(BF16)
        est[mine, :] += tin[...].astype(F32)

    second = core_copy(1, esend, ein)
    second.start()
    second.wait_recv()
    est[theirs, :] = ein[...].astype(F32)

    def out_copy(d):
        return pltpu.make_async_remote_copy(
            src_ref=obuf.at[pl.ds(pl.multiple_of(d * CHUNK, CHUNK), CHUNK)],
            dst_ref=out_hbm.at[:, columns_of(me)],
            send_sem=out_send.at[d],
            recv_sem=out_recv.at[me],
            device_id={"sp": d},
            device_id_type=MESH,
        )

    def finish(b):
        state = (est[...] + upd[b]).astype(BF16)
        numerator = loc[block_rows(b), :] + lax.dot_general(
            qf[b], state, CONTRACT_LAST, preferred_element_type=F32
        )
        scale = lax.rsqrt(jnp.mean(numerator * numerator, -1, keepdims=True) + 1e-06)
        obuf[block_rows(b), :] = (numerator * scale * gain_ref[...]).astype(BF16)

    finish(b0)
    pltpu.make_async_copy(
        obuf.at[pl.ds(pl.multiple_of(me * CHUNK, CHUNK), CHUNK)],
        out_hbm.at[:, columns_of(me)],
        out_recv.at[me],
    ).start()
    out_copy(me + 1 - 2 * lax.rem(me, 2)).start()

    @pl.loop(1, nb)
    def _(i):
        b = lax.rem(b0 + i, nb)
        finish(b)
        for e in range(2):
            out_copy(2 * b + e).start()

    @pl.loop(0, nsp)
    def _(s):
        block = out_hbm.at[:, columns_of(s)]
        pltpu.make_async_copy(block, block, out_recv.at[s]).wait()

    @pl.loop(1, nsp)
    def _(i):
        d = lax.rem(me + i, nsp)
        for t in (K, V, Q):
            input_copy(t, d).wait_send()
        out_copy(d).wait_send()

    for t in (K, V, Q):
        halo_copy(t).wait_send()
    first.wait_send()
    second.wait_send()

    @pl.loop(1, nz)
    def _(i):
        @pl.when(z + i < nz)
        def _():
            z_copy(z + i).wait_send()


def solution(mesh):
    nsp, ngrp = mesh.shape["sp"], mesh.shape["grp"]

    def local(query_input, key_input, value_heads_input, conv_weight, feature_map, out_gain):
        length = nsp * CHUNK
        nb = nsp // 2
        m = feature_map.shape[1]
        any_spec = pl.BlockSpec(memory_space=pl.ANY)
        vmem_spec = pl.BlockSpec(memory_space=pltpu.VMEM)
        dma = pltpu.SemaphoreType.DMA
        return pl.pallas_call(
            functools.partial(kernel, nsp, ngrp),
            out_shape=jax.ShapeDtypeStruct(query_input.shape, BF16),
            in_specs=[any_spec] * 3 + [vmem_spec] * 3,
            out_specs=any_spec,
            scratch_shapes=[
                pltpu.VMEM((HALO + length, DH), BF16),
                pltpu.VMEM((HALO + length, DH), BF16),
                pltpu.VMEM((HALO + length, DH), BF16),
                pltpu.VMEM((nb, BLOCK, m), BF16),
                pltpu.VMEM((nb, BLOCK, m), BF16),
                pltpu.VMEM((length, DH), BF16),
                pltpu.VMEM((nb, DH, m), F32),
                pltpu.VMEM((length, DH), F32),
                pltpu.VMEM((length, DH), BF16),
                pltpu.VMEM((DH, m), F32),
                pltpu.VMEM((DH // 2, m), BF16),
                pltpu.VMEM((DH // 2, m), BF16),
                pltpu.VMEM((DH // 2, m), BF16),
                pltpu.VMEM((ngrp // 2, DH // 2, m), BF16),
                pltpu.VMEM((DH // 2, m), BF16),
                pltpu.VMEM((DH // 2, m), BF16),
                pltpu.VMEM((DH, m), F32),
                dma((3, nsp)),
                dma((3, nsp)),
                dma((3,)),
                dma((3,)),
                dma((2,)),
                dma((2,)),
                dma((ngrp // 2,)),
                dma((ngrp // 2,)),
                dma((nsp,)),
                dma((nsp,)),
            ],
            compiler_params=pltpu.CompilerParams(
                collective_id=0, has_side_effects=True, vmem_limit_bytes=56 << 20
            ),
        )(
            query_input,
            key_input,
            value_heads_input,
            conv_weight,
            feature_map,
            out_gain.reshape(1, DH),
        )

    placed = (
        P(("grp", "sp"), None),
        P(("grp", "sp"), None),
        P(("grp", "sp"), None),
        P(None, None, "sp"),
        P(),
        P("sp"),
    )
    return jax.shard_map(
        local, mesh=mesh, in_specs=placed, out_specs=P(("grp", "sp"), None), check_vma=False
    )
```

```python
import functools

import jax
import jax.numpy as jnp
from jax import lax
from jax.experimental import pallas as pl
from jax.experimental.pallas import tpu as pltpu
from jax.sharding import PartitionSpec as P

DH = 128
CONV = 4
BLOCK = 256
CHUNK = 128
HALO = 16
SLICES = 8
MESH = pl.DeviceIdType.MESH
F32 = jnp.float32
BF16 = jnp.bfloat16
CONTRACT_LAST = (((1,), (1,)), ((), ()))
CONTRACT_FIRST = (((0,), (0,)), ((), ()))
Q, K, V = 0, 1, 2


def kernel(
    nsp,
    ngrp,
    q_hbm,
    k_hbm,
    v_hbm,
    cw_hbm,
    fm_hbm,
    gain_hbm,
    out_hbm,
    qbuf,
    kbuf,
    vbuf,
    qf,
    kf,
    vc,
    upd,
    loc,
    obuf,
    total,
    tsend,
    tin,
    chain_out,
    chain_in,
    pair_out,
    pair_in,
    est,
    cw_ref,
    fm_ref,
    gain_ref,
    in_send,
    in_recv,
    halo_send,
    halo_recv,
    chain_send,
    chain_recv,
    pair_send,
    pair_recv,
    above,
    out_send,
    out_recv,
    weight_sem,
):
    nb = nsp // 2
    m = fm_hbm.shape[1]
    me = lax.axis_index("sp")
    g = lax.axis_index("grp")
    b0 = me // 2
    nz = ngrp // 2
    z, core = g // 2, lax.rem(g, 2)
    partner = g + 1 - 2 * core
    hbm = (q_hbm, k_hbm, v_hbm)
    bufs = (qbuf, kbuf, vbuf)

    barrier = pltpu.get_barrier_semaphore()

    def greet(semaphore, **device):
        pl.semaphore_signal(semaphore, inc=1, device_id=device, device_id_type=MESH)

    @pl.loop(1, nsp)
    def _(i):
        greet(barrier, sp=lax.rem(me + i, nsp))

    greet(barrier, grp=partner)

    @pl.when(g + 2 < ngrp)
    def _():
        greet(barrier, grp=g + 2)

    @pl.when(jnp.logical_and(core == 1, g + 1 < ngrp))
    def _():
        greet(barrier, grp=g + 1)

    weights = [
        pltpu.make_async_copy(src, dst, weight_sem.at[i])
        for i, (src, dst) in enumerate(
            ((cw_hbm, cw_ref), (fm_hbm, fm_ref), (gain_hbm, gain_ref))
        )
    ]
    for copy in weights:
        copy.start()
    pl.semaphore_wait(barrier, nsp + jnp.where(z > 0, 2 - core, 0))

    @pl.when(z > 0)
    def _():
        greet(above, grp=g - 2)

    @pl.when(jnp.logical_and(core == 0, z > 0))
    def _():
        greet(above, grp=g - 1)

    def rows_of(chunk):
        return pl.ds(pl.multiple_of(HALO + chunk * CHUNK, 16), CHUNK)

    def columns_of(head):
        return pl.ds(pl.multiple_of(head * DH, DH), DH)

    def input_copy(t, d):
        return pltpu.make_async_remote_copy(
            src_ref=hbm[t].at[:, columns_of(d)],
            dst_ref=bufs[t].at[rows_of(me)],
            send_sem=in_send.at[t, d],
            recv_sem=in_recv.at[t, me],
            device_id={"sp": d},
            device_id_type=MESH,
        )

    def own_copy(t):
        return pltpu.make_async_copy(
            hbm[t].at[:, columns_of(me)], bufs[t].at[rows_of(me)], in_recv.at[t, me]
        )

    def send_inputs(tensors):
        for t in tensors:
            own_copy(t).start()
        for t in tensors:
            input_copy(t, me + 1 - 2 * lax.rem(me, 2)).start()

        @pl.loop(1, nb)
        def _(i):
            step = jnp.where(b0 == nb - 1, lax.rem(i + nb - 3, nb - 1) + 1, i)
            pair = lax.rem(b0 + nb - step, nb)
            for e in range(2):
                for t in tensors:
                    input_copy(t, 2 * pair + e).start()

    def halo_copy(t):
        return pltpu.make_async_remote_copy(
            src_ref=bufs[t].at[pl.ds(nsp * CHUNK, HALO)],
            dst_ref=bufs[t].at[pl.ds(0, HALO)],
            send_sem=halo_send.at[t],
            recv_sem=halo_recv.at[t],
            device_id={"grp": g + 1},
            device_id_type=MESH,
        )

    def arrive(b, tensors):
        for t in tensors:
            for e in range(2):
                rows = bufs[t].at[rows_of(2 * b + e)]
                pltpu.make_async_copy(rows, rows, in_recv.at[t, 2 * b + e]).wait()

        @pl.when(jnp.logical_and(b == nb - 1, g + 1 < ngrp))
        def _():
            for t in tensors:
                halo_copy(t).start()

    def halo_ready(b, tensors):
        @pl.when(jnp.logical_and(b == 0, g > 0))
        def _():
            for t in tensors:
                halo = bufs[t].at[pl.ds(0, HALO)]
                pltpu.make_async_copy(halo, halo, halo_recv.at[t]).wait()

    def conv(t, b):
        rows = bufs[t][pl.ds(pl.multiple_of(b * BLOCK, BLOCK), BLOCK + HALO), :].astype(F32)
        summed = cw_ref[t, 0:1, :] * rows[HALO:]
        for j in range(1, CONV):
            summed = summed + cw_ref[t, j : j + 1, :] * pltpu.roll(rows, j, 0)[HALO:]
        return summed.astype(BF16)

    def featurize(rows, dst, b):
        for j in range(0, m, 256):
            f = jnp.dot(rows, fm_ref[:, j : j + 256], preferred_element_type=F32)
            dst[b, :, j : j + 256] = jnp.maximum(f, 0.0).astype(BF16)

    def block_rows(b):
        return pl.ds(pl.multiple_of(b * BLOCK, BLOCK), BLOCK)

    send_inputs((K, V))
    send_inputs((Q,))

    @pl.when(g == 0)
    def _():
        for t in (K, V, Q):
            bufs[t][pl.ds(0, HALO), :] = jnp.zeros((HALO, DH), BF16)

    @pl.when(z + 1 < nz)
    def _():
        pl.semaphore_wait(above, 1 + core)

    total[...] = jnp.zeros_like(total)
    for copy in weights:
        copy.wait()

    def key_block(b):
        halo_ready(b, (K, V))
        value = conv(V, b)
        vc[block_rows(b), :] = value
        featurize(conv(K, b), kf, b)
        increment = lax.dot_general(value, kf[b], CONTRACT_FIRST, preferred_element_type=F32)
        upd[b] = increment
        total[...] += increment

    def arrive_first(tensors):
        arrive(b0, tensors)

        @pl.when(b0 == 0)
        def _():
            arrive(nb - 1, tensors)

    def arrive_next(i, b, tensors):
        @pl.when(jnp.logical_or(b0 > 0, i < nb - 1))
        def _():
            arrive(b, tensors)

    arrive_first((K, V))

    @pl.loop(1, nb)
    def _(i):
        b = lax.rem(b0 + i, nb)
        arrive_next(i, b, (K, V))
        key_block(b)

    key_block(b0)

    slices, slice_rows, slice_columns = chain_in.shape
    splits = m // slice_columns
    half = DH // 2

    def place(of, s):
        row = pl.multiple_of(of * half + s // splits * slice_rows, slice_rows)
        column = s % splits * slice_columns
        return pl.ds(row, slice_rows), slice(column, column + slice_columns)

    def pair_copy(k, src, dst):
        return pltpu.make_async_remote_copy(
            src_ref=src,
            dst_ref=dst,
            send_sem=pair_send.at[k],
            recv_sem=pair_recv.at[k],
            device_id={"grp": partner},
            device_id_type=MESH,
        )

    def chain_copy(s):
        return pltpu.make_async_remote_copy(
            src_ref=chain_out.at[s],
            dst_ref=chain_in.at[s],
            send_sem=chain_send.at[s],
            recv_sem=chain_recv.at[s],
            device_id={"grp": g + 2},
            device_id_type=MESH,
        )

    for s in range(slices):
        tsend[s] = total[place(1 - core, s)].astype(BF16)
    first = pair_copy(slices, tsend, tin)
    first.start()

    @pl.when(z == 0)
    def _():
        chain_in[...] = jnp.zeros_like(chain_in)

    def exclusive(b, running):
        increment = upd[b]
        upd[b] = est[...]
        est[...] += increment
        return running

    def exclusive_pass():
        est[...] = jnp.zeros_like(est)
        lax.fori_loop(0, nb, exclusive, 0)

    @pl.when(z >= 3)
    def _():
        exclusive_pass()

    first.wait_recv()
    lower = (1 - core).astype(F32)

    for s in range(slices):

        @pl.when(z > 0)
        def _():
            slot = chain_in.at[s]
            pltpu.make_async_copy(slot, slot, chain_recv.at[s]).wait()

        earlier = chain_in[s].astype(F32)
        own, other = total[place(core, s)], tin[s].astype(F32)

        @pl.when(z + 1 < nz)
        def _():
            chain_out[s] = (earlier + (own + other)).astype(BF16)
            chain_copy(s).start()

        pair_out[s] = (earlier + lower * own).astype(BF16)
        pair_copy(s, pair_out.at[s], pair_in.at[s]).start()

    @pl.when(z < 3)
    def _():
        exclusive_pass()

    for s in range(slices):
        other = tin[s].astype(F32)
        est[place(core, s)] = chain_in[s].astype(F32) + (1.0 - lower) * other

    row_at = lax.broadcasted_iota(jnp.int32, (BLOCK, BLOCK), 0)
    column_at = lax.broadcasted_iota(jnp.int32, (BLOCK, BLOCK), 1)

    def query_block(b):
        halo_ready(b, (Q,))
        featurize(conv(Q, b), qf, b)
        scores = lax.dot_general(qf[b], kf[b], CONTRACT_LAST, preferred_element_type=F32)
        scores = jnp.where(column_at <= row_at, scores, 0.0).astype(BF16)
        loc[block_rows(b), :] = jnp.dot(
            scores, vc[block_rows(b), :], preferred_element_type=F32
        )

    def query_step(i):
        b = lax.rem(b0 + i, nb)
        arrive_next(i, b, (Q,))
        query_block(b)

    arrive_first((Q,))
    for s in range(slices):
        pair_copy(s, pair_out.at[s], pair_in.at[s]).wait_recv()
        est[place(1 - core, s)] = pair_in[s].astype(F32)

    def out_copy(d):
        return pltpu.make_async_remote_copy(
            src_ref=obuf.at[pl.ds(pl.multiple_of(d * CHUNK, CHUNK), CHUNK)],
            dst_ref=out_hbm.at[:, columns_of(me)],
            send_sem=out_send.at[d],
            recv_sem=out_recv.at[me],
            device_id={"sp": d},
            device_id_type=MESH,
        )

    def finish(b):
        state = (est[...] + upd[b]).astype(BF16)
        numerator = loc[block_rows(b), :] + lax.dot_general(
            qf[b], state, CONTRACT_LAST, preferred_element_type=F32
        )
        scale = lax.rsqrt(jnp.mean(numerator * numerator, -1, keepdims=True) + 1e-06)
        obuf[block_rows(b), :] = (numerator * scale * gain_ref[...]).astype(BF16)

    @pl.loop(1, nb)
    def _(i):
        b = lax.rem(b0 + i, nb)
        arrive_next(i, b, (Q,))
        query_block(b)
        finish(b)
        for e in range(2):
            out_copy(2 * b + e).start()

    query_block(b0)
    finish(b0)
    out_copy(me + 1 - 2 * lax.rem(me, 2)).start()
    pltpu.make_async_copy(
        obuf.at[pl.ds(pl.multiple_of(me * CHUNK, CHUNK), CHUNK)],
        out_hbm.at[:, columns_of(me)],
        out_recv.at[me],
    ).start()

    @pl.loop(0, nsp)
    def _(s):
        block = out_hbm.at[:, columns_of(s)]
        pltpu.make_async_copy(block, block, out_recv.at[s]).wait()

    @pl.loop(1, nsp)
    def _(i):
        d = lax.rem(me + i, nsp)
        for t in (K, V, Q):
            input_copy(t, d).wait_send()
        out_copy(d).wait_send()

    @pl.when(g + 1 < ngrp)
    def _():
        for t in (K, V, Q):
            halo_copy(t).wait_send()

    first.wait_send()
    for s in range(slices):
        pair_copy(s, pair_out.at[s], pair_in.at[s]).wait_send()

        @pl.when(z + 1 < nz)
        def _():
            chain_copy(s).wait_send()


def solution(mesh):
    nsp, ngrp = mesh.shape["sp"], mesh.shape["grp"]

    def local(query_input, key_input, value_heads_input, conv_weight, feature_map, out_gain):
        length = nsp * CHUNK
        nb = nsp // 2
        m = feature_map.shape[1]
        pieces = (SLICES, HALO, DH // 2 * m // (HALO * SLICES))
        any_spec = pl.BlockSpec(memory_space=pl.ANY)
        dma = pltpu.SemaphoreType.DMA
        return pl.pallas_call(
            functools.partial(kernel, nsp, ngrp),
            out_shape=jax.ShapeDtypeStruct(query_input.shape, BF16),
            in_specs=[any_spec] * 6,
            out_specs=any_spec,
            scratch_shapes=[
                pltpu.VMEM((HALO + length, DH), BF16),
                pltpu.VMEM((HALO + length, DH), BF16),
                pltpu.VMEM((HALO + length, DH), BF16),
                pltpu.VMEM((nb, BLOCK, m), BF16),
                pltpu.VMEM((nb, BLOCK, m), BF16),
                pltpu.VMEM((length, DH), BF16),
                pltpu.VMEM((nb, DH, m), F32),
                pltpu.VMEM((length, DH), F32),
                pltpu.VMEM((length, DH), BF16),
                pltpu.VMEM((DH, m), F32),
                pltpu.VMEM(pieces, BF16),
                pltpu.VMEM(pieces, BF16),
                pltpu.VMEM(pieces, BF16),
                pltpu.VMEM(pieces, BF16),
                pltpu.VMEM(pieces, BF16),
                pltpu.VMEM(pieces, BF16),
                pltpu.VMEM((DH, m), F32),
                pltpu.VMEM(conv_weight.shape, F32),
                pltpu.VMEM(feature_map.shape, BF16),
                pltpu.VMEM((1, DH), F32),
                dma((3, nsp)),
                dma((3, nsp)),
                dma((3,)),
                dma((3,)),
                dma((SLICES,)),
                dma((SLICES,)),
                dma((SLICES + 1,)),
                dma((SLICES + 1,)),
                pltpu.SemaphoreType.REGULAR,
                dma((nsp,)),
                dma((nsp,)),
                dma((3,)),
            ],
            compiler_params=pltpu.CompilerParams(
                collective_id=0, has_side_effects=True, vmem_limit_bytes=56 << 20
            ),
        )(
            query_input,
            key_input,
            value_heads_input,
            conv_weight,
            feature_map,
            out_gain.reshape(1, DH),
        )

    placed = (
        P(("grp", "sp"), None),
        P(("grp", "sp"), None),
        P(("grp", "sp"), None),
        P(None, None, "sp"),
        P(),
        P("sp"),
    )
    return jax.shard_map(
        local, mesh=mesh, in_specs=placed, out_specs=P(("grp", "sp"), None), check_vma=False
    )
```

```python
import functools

import jax
import jax.numpy as jnp
from jax import lax
from jax.experimental import pallas as pl
from jax.experimental.pallas import tpu as pltpu
from jax.sharding import PartitionSpec as P

DH = 128
CONV = 4
BLOCK = 256
CHUNK = 128
HALO = 16
SLICES = 8
MESH = pl.DeviceIdType.MESH
F32 = jnp.float32
BF16 = jnp.bfloat16
CONTRACT_LAST = (((1,), (1,)), ((), ()))
CONTRACT_FIRST = (((0,), (0,)), ((), ()))
Q, K, V = 0, 1, 2


def kernel(
    nsp,
    ngrp,
    q_hbm,
    k_hbm,
    v_hbm,
    cw_hbm,
    fm_hbm,
    gain_hbm,
    out_hbm,
    qbuf,
    kbuf,
    vbuf,
    qf,
    kf,
    vc,
    upd,
    loc,
    obuf,
    total,
    tsend,
    tin,
    chain_out,
    chain_in,
    pair_out,
    pair_in,
    est,
    cw_ref,
    fm_ref,
    gain_ref,
    in_send,
    in_recv,
    halo_send,
    halo_recv,
    chain_send,
    chain_recv,
    pair_send,
    pair_recv,
    above,
    out_send,
    out_recv,
    weight_sem,
):
    nb = nsp // 2
    m = fm_hbm.shape[1]
    me = lax.axis_index("sp")
    g = lax.axis_index("grp")
    b0 = me // 2
    nz = ngrp // 2
    z, core = g // 2, lax.rem(g, 2)
    partner = g + 1 - 2 * core
    hbm = (q_hbm, k_hbm, v_hbm)
    bufs = (qbuf, kbuf, vbuf)

    barrier = pltpu.get_barrier_semaphore()

    def greet(semaphore, **device):
        pl.semaphore_signal(semaphore, inc=1, device_id=device, device_id_type=MESH)

    @pl.loop(1, nsp)
    def _(i):
        greet(barrier, sp=lax.rem(me + i, nsp))

    greet(barrier, grp=partner)

    @pl.when(g + 2 < ngrp)
    def _():
        greet(barrier, grp=g + 2)

    @pl.when(jnp.logical_and(core == 1, g + 1 < ngrp))
    def _():
        greet(barrier, grp=g + 1)

    weights = [
        pltpu.make_async_copy(src, dst, weight_sem.at[i])
        for i, (src, dst) in enumerate(
            ((cw_hbm, cw_ref), (fm_hbm, fm_ref), (gain_hbm, gain_ref))
        )
    ]
    for copy in weights:
        copy.start()
    pl.semaphore_wait(barrier, nsp + jnp.where(z > 0, 2 - core, 0))

    @pl.when(z > 0)
    def _():
        greet(above, grp=g - 2)

    @pl.when(jnp.logical_and(core == 0, z > 0))
    def _():
        greet(above, grp=g - 1)

    def rows_of(chunk):
        return pl.ds(pl.multiple_of(HALO + chunk * CHUNK, 16), CHUNK)

    def columns_of(head):
        return pl.ds(pl.multiple_of(head * DH, DH), DH)

    def input_copy(t, d):
        return pltpu.make_async_remote_copy(
            src_ref=hbm[t].at[:, columns_of(d)],
            dst_ref=bufs[t].at[rows_of(me)],
            send_sem=in_send.at[t, d],
            recv_sem=in_recv.at[t, me],
            device_id={"sp": d},
            device_id_type=MESH,
        )

    def own_copy(t):
        return pltpu.make_async_copy(
            hbm[t].at[:, columns_of(me)], bufs[t].at[rows_of(me)], in_recv.at[t, me]
        )

    def send_inputs(tensors):
        for t in tensors:
            own_copy(t).start()
        for t in tensors:
            input_copy(t, me + 1 - 2 * lax.rem(me, 2)).start()

        @pl.loop(1, nb)
        def _(i):
            step = jnp.where(b0 == nb - 1, lax.rem(i + nb - 3, nb - 1) + 1, i)
            pair = lax.rem(b0 + nb - step, nb)
            for e in range(2):
                for t in tensors:
                    input_copy(t, 2 * pair + e).start()

    def halo_copy(t):
        return pltpu.make_async_remote_copy(
            src_ref=bufs[t].at[pl.ds(nsp * CHUNK, HALO)],
            dst_ref=bufs[t].at[pl.ds(0, HALO)],
            send_sem=halo_send.at[t],
            recv_sem=halo_recv.at[t],
            device_id={"grp": g + 1},
            device_id_type=MESH,
        )

    def arrive(b, tensors):
        for t in tensors:
            for e in range(2):
                rows = bufs[t].at[rows_of(2 * b + e)]
                pltpu.make_async_copy(rows, rows, in_recv.at[t, 2 * b + e]).wait()

        @pl.when(jnp.logical_and(b == nb - 1, g + 1 < ngrp))
        def _():
            for t in tensors:
                halo_copy(t).start()

    def halo_ready(b, tensors):
        @pl.when(jnp.logical_and(b == 0, g > 0))
        def _():
            for t in tensors:
                halo = bufs[t].at[pl.ds(0, HALO)]
                pltpu.make_async_copy(halo, halo, halo_recv.at[t]).wait()

    def conv(t, b):
        rows = bufs[t][pl.ds(pl.multiple_of(b * BLOCK, BLOCK), BLOCK + HALO), :].astype(F32)
        summed = cw_ref[t, 0:1, :] * rows[HALO:]
        for j in range(1, CONV):
            summed = summed + cw_ref[t, j : j + 1, :] * pltpu.roll(rows, j, 0)[HALO:]
        return summed.astype(BF16)

    def featurize(rows, dst, b):
        for j in range(0, m, 256):
            f = jnp.dot(rows, fm_ref[:, j : j + 256], preferred_element_type=F32)
            dst[b, :, j : j + 256] = jnp.maximum(f, 0.0).astype(BF16)

    def block_rows(b):
        return pl.ds(pl.multiple_of(b * BLOCK, BLOCK), BLOCK)

    send_inputs((K, V))
    send_inputs((Q,))

    @pl.when(g == 0)
    def _():
        for t in (K, V, Q):
            bufs[t][pl.ds(0, HALO), :] = jnp.zeros((HALO, DH), BF16)

    @pl.when(z + 1 < nz)
    def _():
        pl.semaphore_wait(above, 1 + core)

    total[...] = jnp.zeros_like(total)
    for copy in weights:
        copy.wait()

    def key_block(b):
        halo_ready(b, (K, V))
        value = conv(V, b)
        vc[block_rows(b), :] = value
        featurize(conv(K, b), kf, b)
        increment = lax.dot_general(value, kf[b], CONTRACT_FIRST, preferred_element_type=F32)
        upd[b] = increment
        total[...] += increment

    def arrive_first(tensors):
        arrive(b0, tensors)

        @pl.when(b0 == 0)
        def _():
            arrive(nb - 1, tensors)

    def arrive_next(i, b, tensors):
        @pl.when(jnp.logical_or(b0 > 0, i < nb - 1))
        def _():
            arrive(b, tensors)

    arrive_first((K, V))

    @pl.loop(1, nb)
    def _(i):
        b = lax.rem(b0 + i, nb)
        arrive_next(i, b, (K, V))
        key_block(b)

    key_block(b0)

    row_at = lax.broadcasted_iota(jnp.int32, (BLOCK, BLOCK), 0)
    column_at = lax.broadcasted_iota(jnp.int32, (BLOCK, BLOCK), 1)

    def query_block(b):
        halo_ready(b, (Q,))
        featurize(conv(Q, b), qf, b)
        scores = lax.dot_general(qf[b], kf[b], CONTRACT_LAST, preferred_element_type=F32)
        scores = jnp.where(column_at <= row_at, scores, 0.0).astype(BF16)
        loc[block_rows(b), :] = jnp.dot(
            scores, vc[block_rows(b), :], preferred_element_type=F32
        )

    def query_step(i):
        b = lax.rem(b0 + i, nb)
        arrive_next(i, b, (Q,))
        query_block(b)

    slices, slice_rows, slice_columns = chain_in.shape
    splits = m // slice_columns
    half = DH // 2

    def place(of, s):
        row = pl.multiple_of(of * half + s // splits * slice_rows, slice_rows)
        column = s % splits * slice_columns
        return pl.ds(row, slice_rows), slice(column, column + slice_columns)

    def pair_copy(k, src, dst):
        return pltpu.make_async_remote_copy(
            src_ref=src,
            dst_ref=dst,
            send_sem=pair_send.at[k],
            recv_sem=pair_recv.at[k],
            device_id={"grp": partner},
            device_id_type=MESH,
        )

    def chain_copy(s):
        return pltpu.make_async_remote_copy(
            src_ref=chain_out.at[s],
            dst_ref=chain_in.at[s],
            send_sem=chain_send.at[s],
            recv_sem=chain_recv.at[s],
            device_id={"grp": g + 2},
            device_id_type=MESH,
        )

    for s in range(slices):
        tsend[s] = total[place(1 - core, s)].astype(BF16)
    first = pair_copy(slices, tsend, tin)
    first.start()

    @pl.when(z == 0)
    def _():
        chain_in[...] = jnp.zeros_like(chain_in)

    def exclusive(b, running):
        increment = upd[b]
        upd[b] = est[...]
        est[...] += increment
        return running

    def exclusive_pass():
        est[...] = jnp.zeros_like(est)
        lax.fori_loop(0, nb, exclusive, 0)

    @pl.when(z >= 3)
    def _():
        exclusive_pass()

    ahead = jnp.maximum(z - 4, 0) + jnp.where(z == nz - 1, 2, 0)
    arrive_first((Q,))
    pl.loop(1, ahead + 1)(query_step)

    first.wait_recv()
    lower = (1 - core).astype(F32)

    for s in range(slices):

        @pl.when(z > 0)
        def _():
            slot = chain_in.at[s]
            pltpu.make_async_copy(slot, slot, chain_recv.at[s]).wait()

        earlier = chain_in[s].astype(F32)
        own, other = total[place(core, s)], tin[s].astype(F32)

        @pl.when(z + 1 < nz)
        def _():
            chain_out[s] = (earlier + (own + other)).astype(BF16)
            chain_copy(s).start()

        pair_out[s] = (earlier + lower * own).astype(BF16)
        pair_copy(s, pair_out.at[s], pair_in.at[s]).start()

    @pl.when(z < 3)
    def _():
        exclusive_pass()

    for s in range(slices):
        other = tin[s].astype(F32)
        est[place(core, s)] = chain_in[s].astype(F32) + (1.0 - lower) * other

    for s in range(slices):
        pair_copy(s, pair_out.at[s], pair_in.at[s]).wait_recv()
        est[place(1 - core, s)] = pair_in[s].astype(F32)

    def out_copy(d):
        return pltpu.make_async_remote_copy(
            src_ref=obuf.at[pl.ds(pl.multiple_of(d * CHUNK, CHUNK), CHUNK)],
            dst_ref=out_hbm.at[:, columns_of(me)],
            send_sem=out_send.at[d],
            recv_sem=out_recv.at[me],
            device_id={"sp": d},
            device_id_type=MESH,
        )

    def finish(b):
        state = (est[...] + upd[b]).astype(BF16)
        numerator = loc[block_rows(b), :] + lax.dot_general(
            qf[b], state, CONTRACT_LAST, preferred_element_type=F32
        )
        scale = lax.rsqrt(jnp.mean(numerator * numerator, -1, keepdims=True) + 1e-06)
        obuf[block_rows(b), :] = (numerator * scale * gain_ref[...]).astype(BF16)

    @pl.loop(1, nb)
    def _(i):
        b = lax.rem(b0 + i, nb)

        @pl.when(i > ahead)
        def _():
            query_step(i)

        finish(b)
        for e in range(2):
            out_copy(2 * b + e).start()

    query_block(b0)
    finish(b0)
    out_copy(me + 1 - 2 * lax.rem(me, 2)).start()
    pltpu.make_async_copy(
        obuf.at[pl.ds(pl.multiple_of(me * CHUNK, CHUNK), CHUNK)],
        out_hbm.at[:, columns_of(me)],
        out_recv.at[me],
    ).start()

    @pl.loop(0, nsp)
    def _(s):
        block = out_hbm.at[:, columns_of(s)]
        pltpu.make_async_copy(block, block, out_recv.at[s]).wait()

    @pl.loop(1, nsp)
    def _(i):
        d = lax.rem(me + i, nsp)
        for t in (K, V, Q):
            input_copy(t, d).wait_send()
        out_copy(d).wait_send()

    @pl.when(g + 1 < ngrp)
    def _():
        for t in (K, V, Q):
            halo_copy(t).wait_send()

    first.wait_send()
    for s in range(slices):
        pair_copy(s, pair_out.at[s], pair_in.at[s]).wait_send()

        @pl.when(z + 1 < nz)
        def _():
            chain_copy(s).wait_send()


def solution(mesh):
    nsp, ngrp = mesh.shape["sp"], mesh.shape["grp"]

    def local(query_input, key_input, value_heads_input, conv_weight, feature_map, out_gain):
        length = nsp * CHUNK
        nb = nsp // 2
        m = feature_map.shape[1]
        pieces = (SLICES, HALO, DH // 2 * m // (HALO * SLICES))
        any_spec = pl.BlockSpec(memory_space=pl.ANY)
        dma = pltpu.SemaphoreType.DMA
        return pl.pallas_call(
            functools.partial(kernel, nsp, ngrp),
            out_shape=jax.ShapeDtypeStruct(query_input.shape, BF16),
            in_specs=[any_spec] * 6,
            out_specs=any_spec,
            scratch_shapes=[
                pltpu.VMEM((HALO + length, DH), BF16),
                pltpu.VMEM((HALO + length, DH), BF16),
                pltpu.VMEM((HALO + length, DH), BF16),
                pltpu.VMEM((nb, BLOCK, m), BF16),
                pltpu.VMEM((nb, BLOCK, m), BF16),
                pltpu.VMEM((length, DH), BF16),
                pltpu.VMEM((nb, DH, m), F32),
                pltpu.VMEM((length, DH), F32),
                pltpu.VMEM((length, DH), BF16),
                pltpu.VMEM((DH, m), F32),
                pltpu.VMEM(pieces, BF16),
                pltpu.VMEM(pieces, BF16),
                pltpu.VMEM(pieces, BF16),
                pltpu.VMEM(pieces, BF16),
                pltpu.VMEM(pieces, BF16),
                pltpu.VMEM(pieces, BF16),
                pltpu.VMEM((DH, m), F32),
                pltpu.VMEM(conv_weight.shape, F32),
                pltpu.VMEM(feature_map.shape, BF16),
                pltpu.VMEM((1, DH), F32),
                dma((3, nsp)),
                dma((3, nsp)),
                dma((3,)),
                dma((3,)),
                dma((SLICES,)),
                dma((SLICES,)),
                dma((SLICES + 1,)),
                dma((SLICES + 1,)),
                pltpu.SemaphoreType.REGULAR,
                dma((nsp,)),
                dma((nsp,)),
                dma((3,)),
            ],
            compiler_params=pltpu.CompilerParams(
                collective_id=0, has_side_effects=True, vmem_limit_bytes=52 << 20
            ),
        )(
            query_input,
            key_input,
            value_heads_input,
            *(
                pltpu.with_memory_space_constraint(w, pltpu.HBM)
                for w in (conv_weight, feature_map, out_gain.reshape(1, DH))
            ),
        )

    placed = (
        P(("grp", "sp"), None),
        P(("grp", "sp"), None),
        P(("grp", "sp"), None),
        P(None, None, "sp"),
        P(),
        P("sp"),
    )
    return jax.shard_map(
        local, mesh=mesh, in_specs=placed, out_specs=P(("grp", "sp"), None), check_vma=False
    )
```

```python
import functools

import jax
import jax.numpy as jnp
from jax import lax
from jax.experimental import pallas as pl
from jax.experimental.pallas import tpu as pltpu
from jax.sharding import PartitionSpec as P

DH = 128
CONV = 4
BLOCK = 256
CHUNK = 128
HALO = 16
SLICES = 8
MESH = pl.DeviceIdType.MESH
F32 = jnp.float32
BF16 = jnp.bfloat16
CONTRACT_LAST = (((1,), (1,)), ((), ()))
CONTRACT_FIRST = (((0,), (0,)), ((), ()))
Q, K, V = 0, 1, 2


def kernel(
    nsp,
    ngrp,
    q_hbm,
    k_hbm,
    v_hbm,
    cw_hbm,
    fm_hbm,
    gain_hbm,
    out_hbm,
    qbuf,
    kbuf,
    vbuf,
    qf,
    kf,
    vc,
    upd,
    loc,
    obuf,
    total,
    tsend,
    tin,
    chain_out,
    chain_in,
    pair_out,
    pair_in,
    est,
    cw_ref,
    fm_ref,
    gain_ref,
    in_send,
    in_recv,
    halo_send,
    halo_recv,
    chain_send,
    chain_recv,
    pair_send,
    pair_recv,
    above,
    out_send,
    out_recv,
    weight_sem,
):
    nb = nsp // 2
    m = fm_hbm.shape[1]
    me = lax.axis_index("sp")
    g = lax.axis_index("grp")
    b0 = me // 2
    nz = ngrp // 2
    z, core = g // 2, lax.rem(g, 2)
    partner = g + 1 - 2 * core
    hbm = (q_hbm, k_hbm, v_hbm)
    bufs = (qbuf, kbuf, vbuf)

    barrier = pltpu.get_barrier_semaphore()

    def greet(semaphore, **device):
        pl.semaphore_signal(semaphore, inc=1, device_id=device, device_id_type=MESH)

    @pl.loop(1, nsp)
    def _(i):
        greet(barrier, sp=lax.rem(me + i, nsp))

    greet(barrier, grp=partner)

    @pl.when(g + 2 < ngrp)
    def _():
        greet(barrier, grp=g + 2)

    @pl.when(jnp.logical_and(core == 1, g + 1 < ngrp))
    def _():
        greet(barrier, grp=g + 1)

    weights = [
        pltpu.make_async_copy(src, dst, weight_sem.at[i])
        for i, (src, dst) in enumerate(
            ((cw_hbm, cw_ref), (fm_hbm, fm_ref), (gain_hbm, gain_ref))
        )
    ]
    for copy in weights:
        copy.start()
    pl.semaphore_wait(barrier, nsp + jnp.where(z > 0, 2 - core, 0))

    @pl.when(z > 0)
    def _():
        greet(above, grp=g - 2)

    @pl.when(jnp.logical_and(core == 0, z > 0))
    def _():
        greet(above, grp=g - 1)

    def rows_of(chunk):
        return pl.ds(pl.multiple_of(HALO + chunk * CHUNK, 16), CHUNK)

    def columns_of(head):
        return pl.ds(pl.multiple_of(head * DH, DH), DH)

    def input_copy(t, d):
        return pltpu.make_async_remote_copy(
            src_ref=hbm[t].at[:, columns_of(d)],
            dst_ref=bufs[t].at[rows_of(me)],
            send_sem=in_send.at[t, d],
            recv_sem=in_recv.at[t, me],
            device_id={"sp": d},
            device_id_type=MESH,
        )

    def own_copy(t):
        return pltpu.make_async_copy(
            hbm[t].at[:, columns_of(me)], bufs[t].at[rows_of(me)], in_recv.at[t, me]
        )

    def send_inputs(tensors):
        for t in tensors:
            own_copy(t).start()
        for t in tensors:
            input_copy(t, me + 1 - 2 * lax.rem(me, 2)).start()

        @pl.loop(1, nb)
        def _(i):
            step = jnp.where(b0 == nb - 1, lax.rem(i + nb - 3, nb - 1) + 1, i)
            pair = lax.rem(b0 + nb - step, nb)
            for e in range(2):
                for t in tensors:
                    input_copy(t, 2 * pair + e).start()

    def halo_copy(t):
        return pltpu.make_async_remote_copy(
            src_ref=bufs[t].at[pl.ds(nsp * CHUNK, HALO)],
            dst_ref=bufs[t].at[pl.ds(0, HALO)],
            send_sem=halo_send.at[t],
            recv_sem=halo_recv.at[t],
            device_id={"grp": g + 1},
            device_id_type=MESH,
        )

    def arrive(b, tensors):
        for t in tensors:
            for e in range(2):
                rows = bufs[t].at[rows_of(2 * b + e)]
                pltpu.make_async_copy(rows, rows, in_recv.at[t, 2 * b + e]).wait()

        @pl.when(jnp.logical_and(b == nb - 1, g + 1 < ngrp))
        def _():
            for t in tensors:
                halo_copy(t).start()

    def halo_ready(b, tensors):
        @pl.when(jnp.logical_and(b == 0, g > 0))
        def _():
            for t in tensors:
                halo = bufs[t].at[pl.ds(0, HALO)]
                pltpu.make_async_copy(halo, halo, halo_recv.at[t]).wait()

    def conv(t, b):
        rows = bufs[t][pl.ds(pl.multiple_of(b * BLOCK, BLOCK), BLOCK + HALO), :].astype(F32)
        summed = cw_ref[t, 0:1, :] * rows[HALO:]
        for j in range(1, CONV):
            summed = summed + cw_ref[t, j : j + 1, :] * pltpu.roll(rows, j, 0)[HALO:]
        return summed.astype(BF16)

    def featurize(rows, dst, b):
        for j in range(0, m, 256):
            f = jnp.dot(rows, fm_ref[:, j : j + 256], preferred_element_type=F32)
            dst[b, :, j : j + 256] = jnp.maximum(f, 0.0).astype(BF16)

    def block_rows(b):
        return pl.ds(pl.multiple_of(b * BLOCK, BLOCK), BLOCK)

    send_inputs((K, V))
    send_inputs((Q,))

    @pl.when(g == 0)
    def _():
        for t in (K, V, Q):
            bufs[t][pl.ds(0, HALO), :] = jnp.zeros((HALO, DH), BF16)

    @pl.when(z + 1 < nz)
    def _():
        pl.semaphore_wait(above, 1 + core)

    total[...] = jnp.zeros_like(total)
    for copy in weights:
        copy.wait()

    def key_block(b):
        halo_ready(b, (K, V))
        value = conv(V, b)
        vc[block_rows(b), :] = value
        featurize(conv(K, b), kf, b)
        increment = lax.dot_general(value, kf[b], CONTRACT_FIRST, preferred_element_type=F32)
        upd[b] = increment
        total[...] += increment

    def arrive_first(tensors):
        arrive(b0, tensors)

        @pl.when(b0 == 0)
        def _():
            arrive(nb - 1, tensors)

    def arrive_next(i, b, tensors):
        @pl.when(jnp.logical_or(b0 > 0, i < nb - 1))
        def _():
            arrive(b, tensors)

    arrive_first((K, V))

    @pl.loop(1, nb)
    def _(i):
        b = lax.rem(b0 + i, nb)
        arrive_next(i, b, (K, V))
        key_block(b)

    key_block(b0)

    row_at = lax.broadcasted_iota(jnp.int32, (BLOCK, BLOCK), 0)
    column_at = lax.broadcasted_iota(jnp.int32, (BLOCK, BLOCK), 1)

    def query_block(b):
        halo_ready(b, (Q,))
        featurize(conv(Q, b), qf, b)
        scores = lax.dot_general(qf[b], kf[b], CONTRACT_LAST, preferred_element_type=F32)
        scores = jnp.where(column_at <= row_at, scores, 0.0).astype(BF16)
        loc[block_rows(b), :] = jnp.dot(
            scores, vc[block_rows(b), :], preferred_element_type=F32
        )

    def query_step(i):
        b = lax.rem(b0 + i, nb)
        arrive_next(i, b, (Q,))
        query_block(b)

    slices, slice_rows, slice_columns = chain_in.shape
    splits = m // slice_columns
    half = DH // 2

    def place(of, s):
        row = pl.multiple_of(of * half + s // splits * slice_rows, slice_rows)
        column = s % splits * slice_columns
        return pl.ds(row, slice_rows), slice(column, column + slice_columns)

    def pair_copy(k, src, dst):
        return pltpu.make_async_remote_copy(
            src_ref=src,
            dst_ref=dst,
            send_sem=pair_send.at[k],
            recv_sem=pair_recv.at[k],
            device_id={"grp": partner},
            device_id_type=MESH,
        )

    def chain_copy(s):
        return pltpu.make_async_remote_copy(
            src_ref=chain_out.at[s],
            dst_ref=chain_in.at[s],
            send_sem=chain_send.at[s],
            recv_sem=chain_recv.at[s],
            device_id={"grp": g + 2},
            device_id_type=MESH,
        )

    for s in range(slices):
        tsend[s] = total[place(1 - core, s)].astype(BF16)
    first = pair_copy(slices, tsend, tin)
    first.start()

    @pl.when(z == 0)
    def _():
        chain_in[...] = jnp.zeros_like(chain_in)

    def exclusive(b, running):
        increment = upd[b]
        upd[b] = est[...]
        est[...] += increment
        return running

    def exclusive_pass():
        est[...] = jnp.zeros_like(est)
        lax.fori_loop(0, nb, exclusive, 0)

    @pl.when(z >= 3)
    def _():
        exclusive_pass()

    ahead = jnp.where(z == nz - 1, 2, 0)
    arrive_first((Q,))
    pl.loop(1, ahead + 1)(query_step)

    first.wait_recv()
    lower = (1 - core).astype(F32)

    for s in range(slices):

        @pl.when(z > 0)
        def _():
            slot = chain_in.at[s]
            pltpu.make_async_copy(slot, slot, chain_recv.at[s]).wait()

        earlier = chain_in[s].astype(F32)
        own, other = total[place(core, s)], tin[s].astype(F32)

        @pl.when(z + 1 < nz)
        def _():
            chain_out[s] = (earlier + (own + other)).astype(BF16)
            chain_copy(s).start()

        pair_out[s] = (earlier + lower * own).astype(BF16)
        pair_copy(s, pair_out.at[s], pair_in.at[s]).start()

    @pl.when(z < 3)
    def _():
        exclusive_pass()

    for s in range(slices):
        other = tin[s].astype(F32)
        est[place(core, s)] = chain_in[s].astype(F32) + (1.0 - lower) * other

    done = ahead + 2
    pl.loop(ahead + 1, done + 1)(query_step)

    for s in range(slices):
        pair_copy(s, pair_out.at[s], pair_in.at[s]).wait_recv()
        est[place(1 - core, s)] = pair_in[s].astype(F32)

    def out_copy(d):
        return pltpu.make_async_remote_copy(
            src_ref=obuf.at[pl.ds(pl.multiple_of(d * CHUNK, CHUNK), CHUNK)],
            dst_ref=out_hbm.at[:, columns_of(me)],
            send_sem=out_send.at[d],
            recv_sem=out_recv.at[me],
            device_id={"sp": d},
            device_id_type=MESH,
        )

    def finish(b):
        state = (est[...] + upd[b]).astype(BF16)
        numerator = loc[block_rows(b), :] + lax.dot_general(
            qf[b], state, CONTRACT_LAST, preferred_element_type=F32
        )
        scale = lax.rsqrt(jnp.mean(numerator * numerator, -1, keepdims=True) + 1e-06)
        obuf[block_rows(b), :] = (numerator * scale * gain_ref[...]).astype(BF16)

    @pl.loop(1, nb)
    def _(i):
        b = lax.rem(b0 + i, nb)

        @pl.when(i > done)
        def _():
            query_step(i)

        finish(b)
        for e in range(2):
            out_copy(2 * b + e).start()

    query_block(b0)
    finish(b0)
    out_copy(me + 1 - 2 * lax.rem(me, 2)).start()
    pltpu.make_async_copy(
        obuf.at[pl.ds(pl.multiple_of(me * CHUNK, CHUNK), CHUNK)],
        out_hbm.at[:, columns_of(me)],
        out_recv.at[me],
    ).start()

    @pl.loop(0, nsp)
    def _(s):
        block = out_hbm.at[:, columns_of(s)]
        pltpu.make_async_copy(block, block, out_recv.at[s]).wait()

    @pl.loop(1, nsp)
    def _(i):
        d = lax.rem(me + i, nsp)
        for t in (K, V, Q):
            input_copy(t, d).wait_send()
        out_copy(d).wait_send()

    @pl.when(g + 1 < ngrp)
    def _():
        for t in (K, V, Q):
            halo_copy(t).wait_send()

    first.wait_send()
    for s in range(slices):
        pair_copy(s, pair_out.at[s], pair_in.at[s]).wait_send()

        @pl.when(z + 1 < nz)
        def _():
            chain_copy(s).wait_send()


def solution(mesh):
    nsp, ngrp = mesh.shape["sp"], mesh.shape["grp"]

    def local(query_input, key_input, value_heads_input, conv_weight, feature_map, out_gain):
        length = nsp * CHUNK
        nb = nsp // 2
        m = feature_map.shape[1]
        pieces = (SLICES, HALO, DH // 2 * m // (HALO * SLICES))
        any_spec = pl.BlockSpec(memory_space=pl.ANY)
        dma = pltpu.SemaphoreType.DMA
        return pl.pallas_call(
            functools.partial(kernel, nsp, ngrp),
            out_shape=jax.ShapeDtypeStruct(query_input.shape, BF16),
            in_specs=[any_spec] * 6,
            out_specs=any_spec,
            scratch_shapes=[
                pltpu.VMEM((HALO + length, DH), BF16),
                pltpu.VMEM((HALO + length, DH), BF16),
                pltpu.VMEM((HALO + length, DH), BF16),
                pltpu.VMEM((nb, BLOCK, m), BF16),
                pltpu.VMEM((nb, BLOCK, m), BF16),
                pltpu.VMEM((length, DH), BF16),
                pltpu.VMEM((nb, DH, m), F32),
                pltpu.VMEM((length, DH), F32),
                pltpu.VMEM((length, DH), BF16),
                pltpu.VMEM((DH, m), F32),
                pltpu.VMEM(pieces, BF16),
                pltpu.VMEM(pieces, BF16),
                pltpu.VMEM(pieces, BF16),
                pltpu.VMEM(pieces, BF16),
                pltpu.VMEM(pieces, BF16),
                pltpu.VMEM(pieces, BF16),
                pltpu.VMEM((DH, m), F32),
                pltpu.VMEM(conv_weight.shape, F32),
                pltpu.VMEM(feature_map.shape, BF16),
                pltpu.VMEM((1, DH), F32),
                dma((3, nsp)),
                dma((3, nsp)),
                dma((3,)),
                dma((3,)),
                dma((SLICES,)),
                dma((SLICES,)),
                dma((SLICES + 1,)),
                dma((SLICES + 1,)),
                pltpu.SemaphoreType.REGULAR,
                dma((nsp,)),
                dma((nsp,)),
                dma((3,)),
            ],
            compiler_params=pltpu.CompilerParams(
                collective_id=0, has_side_effects=True, vmem_limit_bytes=52 << 20
            ),
        )(
            query_input,
            key_input,
            value_heads_input,
            *(
                pltpu.with_memory_space_constraint(w, pltpu.HBM)
                for w in (conv_weight, feature_map, out_gain.reshape(1, DH))
            ),
        )

    placed = (
        P(("grp", "sp"), None),
        P(("grp", "sp"), None),
        P(("grp", "sp"), None),
        P(None, None, "sp"),
        P(),
        P("sp"),
    )
    return jax.shard_map(
        local, mesh=mesh, in_specs=placed, out_specs=P(("grp", "sp"), None), check_vma=False
    )
```
